256 devices in a mesh: tm: 64 (over x, z_lo, y), space: 4 (over z_hi, core).
Axes of the slice: x: 4, y: 4, z: 8 (z_hi: 2, z_lo: 4; z = z_hi * 4 + z_lo), core: 2. Of those that a mesh axis runs over, the one named last changes fastest.
Arguments:
- start: float32 [64, 2, 32, 64, 128], P('tm', None, 'space'), may hold values from -0.2 to 1.2
- conduct: float32 [32, 64, 128], P('space'), may hold values from 0.03 to 0.12
- threshold: float32 [32, 64, 128], P('space'), may hold values from 0.05 to 0.45
- recovery: float32 [32, 64, 128], P('space'), may hold values from 0.02 to 0.3
Outputs:
- final: float32 [64, 2, 32, 64, 128], P('tm', None, 'space')
The draws below stay inside these ranges and needn't reach their ends.
All inputs are finite; a program needn't handle non-finite values.
Results may differ from the reference program's by a relative error of at most 0.0001.
Values sent between devices are 32-bit elements; how exact they have to be, the bound alone decides.
No kernel may reach another device: no remote copies, remote signals or barrier semaphores. Data moves between devices by JAX's collectives and lax.ppermute only.
A program may use at most 64 MiB of HBM per device.

```python
import math
import jax
import jax.numpy as jnp
from jax import lax

NY = 64
NZ = 128
ITERS = 2
SLICES = 64
NX = 32


def shard_levels(own_key, shape, split, smallest, high):
    def one(position, shards_of):
        draws = jax.random.uniform(jax.random.fold_in(jax.random.fold_in(own_key, 6), position), (shards_of,), jnp.float32, smallest / len(split), high / len(split))
        return jnp.repeat(jnp.exp(draws), shape[position] // shards_of).reshape((-1,) + (1,) * (len(shape) - position - 1))

    gain = one(*split[0])
    for cut in split[1:]:
        gain = gain * one(*cut)
    return gain


def setup_inputs(seed: int = 0) -> dict:
    streams_of = jax.random.split(jax.random.key(seed), 5)
    return {
        "start": jnp.clip(-0.2 + 1.4000001 * jax.random.uniform(streams_of[0], (SLICES, 2, NX, NY, NZ), jnp.float32) ** shard_levels(streams_of[0], (SLICES, 2, NX, NY, NZ), ((0, 64), (2, 4)), -0.2, 0.2), -0.2, 1.2),
        "conduct": jnp.clip(jnp.exp(math.log(0.12) - 1.3862944 * jax.random.uniform(streams_of[1], (NX, NY, NZ), jnp.float32) ** shard_levels(streams_of[1], (NX, NY, NZ), ((0, 4),), -0.2, 0.2)), 0.03, 0.12),
        "threshold": jnp.clip(0.05 + 0.39999999 * jax.random.uniform(streams_of[2], (NX, NY, NZ), jnp.float32) ** shard_levels(streams_of[2], (NX, NY, NZ), ((0, 4),), -0.2, 0.2), 0.05, 0.45),
        "recovery": jnp.clip(jnp.exp(math.log(0.3) - 2.7080503 * jax.random.uniform(streams_of[3], (NX, NY, NZ), jnp.float32) ** shard_levels(streams_of[3], (NX, NY, NZ), ((0, 4),), -0.2, 0.2)), 0.02, 0.3),
    }


quad_first = (5.0 / 24.0, 1.0 / 3.0, -1.0 / 24.0)
quad_second = (-1.0 / 24.0, 1.0 / 3.0, 5.0 / 24.0)
node_step = 0.5
reaction = 2.0
recovery_ratio = 0.5


def quadrature(weights, terms):
    return weights[0] * terms[0] + weights[1] * terms[1] + weights[2] * terms[2]


def fine_laplace(padded, values):
    summed = padded[:, 2:, 1:-1, 1:-1] + padded[:, :-2, 1:-1, 1:-1]
    summed = summed + padded[:, 1:-1, 2:, 1:-1] + padded[:, 1:-1, :-2, 1:-1]
    summed = summed + padded[:, 1:-1, 1:-1, 2:] + padded[:, 1:-1, 1:-1, :-2]
    return summed - 6.0 * values


def coarse_laplace(padded, values):
    along_x = padded[:, 2:, 1:-1, 1:-1] + padded[:, :-2, 1:-1, 1:-1] - 2.0 * values
    along_y = padded[:, 1:-1, 2:, 1:-1] + padded[:, 1:-1, :-2, 1:-1] - 2.0 * values
    along_z = padded[:, 1:-1, 1:-1, 2:] + padded[:, 1:-1, 1:-1, :-2] - 2.0 * values
    return 0.25 * along_x + 0.25 * along_y + along_z


def forces(states, laplace, coeffs):
    conduct, threshold, recovery = coeffs
    excite = states[:, 0]
    slower = states[:, 1]
    driving = conduct * laplace + reaction * excite * (1.0 - excite) * (excite - threshold) - slower
    relaxing = recovery * (excite - recovery_ratio * slower)
    return jnp.stack([driving, relaxing], axis=1)


def restrict(values):
    sizes_of = values.shape
    blocks = values.reshape(sizes_of[:-3] + (sizes_of[-3] // 2, 2, sizes_of[-2] // 2, 2, sizes_of[-1]))
    return 0.25 * jnp.sum(blocks, axis=(-4, -2))


def prolong(values):
    sizes_of = values.shape
    widened = jnp.broadcast_to(values[..., :, None, :, None, :], sizes_of[:-3] + (sizes_of[-3], 2, sizes_of[-2], 2, sizes_of[-1]))
    return widened.reshape(sizes_of[:-3] + (2 * sizes_of[-3], 2 * sizes_of[-2], sizes_of[-1]))


def fine_all(states, coeffs):
    padded = jnp.pad(states[:, 0], ((0, 0), (1, 1), (1, 1), (1, 1)))
    return forces(states, fine_laplace(padded, states[:, 0]), coeffs)


def coarse_all(states, coeffs):
    padded = jnp.pad(states[:, 0], ((0, 0), (1, 1), (1, 1), (1, 1)))
    return forces(states, coarse_laplace(padded, states[:, 0]), coeffs)


def slice_pass(nodes, initial, fine_coeffs, coarse_coeffs):
    old_terms = fine_all(nodes, fine_coeffs)
    term_zero = fine_all(initial[None], fine_coeffs)[0]
    node_one = initial + node_step * (term_zero - old_terms[0]) + quadrature(quad_first, old_terms)
    term_one = fine_all(node_one[None], fine_coeffs)[0]
    node_two = node_one + node_step * (term_one - old_terms[1]) + quadrature(quad_second, old_terms)
    term_two = fine_all(node_two[None], fine_coeffs)[0]
    new_terms = (term_zero, term_one, term_two)
    sum_first = quadrature(quad_first, new_terms)
    sum_second = quadrature(quad_second, new_terms)
    coarse_zero = restrict(initial)
    base_one = restrict(node_one)
    coarse_one = coarse_zero + restrict(sum_first)
    pair_terms = coarse_all(jnp.stack([base_one, coarse_one]), coarse_coeffs)
    coarse_two = coarse_one + node_step * (pair_terms[1] - pair_terms[0]) + restrict(sum_second)
    node_one_new = node_one + prolong(coarse_one - base_one)
    node_two_new = node_two + prolong(coarse_two - restrict(node_two))
    return jnp.stack([initial, node_one_new, node_two_new])


def reference(start, conduct, threshold, recovery):
    fine_coeffs = (conduct, threshold, recovery)
    coarse_coeffs = (restrict(conduct), restrict(threshold), restrict(recovery))
    nodes = jnp.broadcast_to(start[:, None], (SLICES, 3) + start.shape[1:])
    initials = start

    def one_slice(carried):
        return slice_pass(carried[0], carried[1], fine_coeffs, coarse_coeffs)

    for sweep_index in range(ITERS):
        nodes = lax.map(one_slice, (nodes, initials))
        initials = jnp.concatenate([start[:1], nodes[:-1, 2]], axis=0)
    return nodes[:, 2]
```

```python
import functools

import jax
import jax.numpy as jnp
from jax import lax
from jax.experimental import pallas as pl
from jax.experimental.pallas import tpu as pltpu
from jax.sharding import PartitionSpec as P

F32 = jnp.float32
H = 0.5
SLAB = 8
NY = 64
NZ = 128
PLANE = (NY, NZ)
ROWS = NY // 2

VM = pl.BlockSpec(memory_space=pltpu.VMEM)
SM = pl.BlockSpec(memory_space=pltpu.SMEM)
ANY = pl.BlockSpec(memory_space=pl.ANY)


def planes(count, rows=NY):
    return jax.ShapeDtypeStruct((count, rows, NZ), F32)


def grid_masks():
    row = lax.broadcasted_iota(jnp.int32, PLANE, 0)
    lane = lax.broadcasted_iota(jnp.int32, PLANE, 1)
    return row, lane


def shift_rows(v, by, row):
    rolled = pltpu.roll(v, (-by) % NY, 0)
    if by > 0:
        return jnp.where(row < NY - by, rolled, 0.0)
    return jnp.where(row >= -by, rolled, 0.0)


def shift_lanes(v, by, lane):
    rolled = pltpu.roll(v, (-by) % NZ, 1)
    if by > 0:
        return jnp.where(lane < NZ - by, rolled, 0.0)
    return jnp.where(lane >= -by, rolled, 0.0)


def fine_laplace(before, here, after, masks):
    row, lane = masks
    total = before + after
    total = total + (shift_rows(here, 1, row) + shift_rows(here, -1, row))
    total = total + (shift_lanes(here, 1, lane) + shift_lanes(here, -1, lane))
    return total - 6.0 * here


def driving(before, here, after, slow, conduct, threshold, masks):
    local = 2.0 * here * (1.0 - here) * (here - threshold) - slow
    return conduct * fine_laplace(before, here, after, masks) + local


def relaxing(here, slow, recovery):
    return recovery * (here - 0.5 * slow)


def pair_mean(v, row):
    other = jnp.where(row % 2 == 0, pltpu.roll(v, NY - 1, 0), pltpu.roll(v, 1, 0))
    return 0.25 * (v + other)


def coarse_laplace_inside(here, masks):
    row, lane = masks
    along_y = shift_rows(here, 2, row) + shift_rows(here, -2, row) - 2.0 * here
    along_z = shift_lanes(here, 1, lane) + shift_lanes(here, -1, lane) - 2.0 * here
    return 0.25 * along_y + along_z - 0.5 * here


def loop(count, body):
    def step(i, carry):
        body(i)
        return carry

    lax.fori_loop(0, count, step, 0)


def pack_kernel(core_ref, start, conduct, threshold, recovery, to_a, to_b, sem):
    core = core_ref[0]
    moves = []
    for pay, right in ((to_a, core == 0), (to_b, core == 1)):
        at = 0
        for src, width in (
            (start.at[0, 0], 5),
            (start.at[0, 1], 4),
            (conduct, 4),
            (threshold, 4),
            (recovery, 3),
        ):
            off = jnp.where(right, SLAB - width, 0)
            moves.append(
                pltpu.make_async_copy(
                    src.at[pl.ds(off, width)], pay.at[pl.ds(at, width)], sem.at[len(moves)]
                )
            )
            at += width
    for move in moves:
        move.start()
    for move in moves:
        move.wait()


def copy_planes(dst, at, src, first, count):
    dst[pl.ds(at, count)] = src[pl.ds(first, count)]


def sides(core, ra, rb, fill):
    @pl.when(core == 0)
    def _():
        fill(rb, ra)

    @pl.when(core == 1)
    def _():
        fill(ra, rb)


def first_kernel(
    core_ref, start, conduct, threshold, recovery, ra, rb,
    u2, dpay, bpay, apay, e, r, c, th, rc, f0e, f0r, n1e, n1r, n2e, n2r, d1e, d1r, dle, dlr,
    f1e, f1r, rse, rsr, line,
):
    core = core_ref[0]
    masks = grid_masks()
    row = masks[0]
    for dst, at, src in ((e, 5, start.at[0, 0]), (r, 4, start.at[0, 1]), (c, 4, conduct), (th, 4, threshold), (rc, 4, recovery)):
        copy_planes(dst, at, src, 0, SLAB)

    def fill(left, right):
        for halo, hi in ((left, False), (right, True)):
            copy_planes(e, 13 if hi else 0, halo, 0, 5)
            copy_planes(r, 12 if hi else 0, halo, 5, 4)
            copy_planes(c, 12 if hi else 0, halo, 9, 4)
            copy_planes(th, 12 if hi else 0, halo, 13, 4)
            copy_planes(rc, 12 if hi else 1, halo, 17, 3)

    sides(core, ra, rb, fill)
    rc[0] = jnp.zeros(PLANE, F32)
    rc[15] = jnp.zeros(PLANE, F32)

    def one(i):
        here, slow = e[i + 1], r[i]
        fe = driving(e[i], here, e[i + 2], slow, c[i], th[i], masks)
        fr = relaxing(here, slow, rc[i])
        f0e[i] = fe
        f0r[i] = fr
        n1e[i] = here + H * fe
        n1r[i] = slow + H * fr

    loop(16, one)

    def two(i):
        here, slow = n1e[i + 1], n1r[i + 1]
        fe = driving(n1e[i], here, n1e[i + 2], slow, c[i + 1], th[i + 1], masks)
        fr = relaxing(here, slow, rc[i + 1])
        f1e[i] = fe
        f1r[i] = fr
        n2e[i] = here + H * fe
        n2r[i] = slow + H * fr

    loop(14, two)

    def three(k):
        jump_e = jump_r = sum_e = sum_r = 0.0
        for half in range(2):
            i = 2 * k + half
            here, slow = n2e[i + 1], n2r[i + 1]
            fe = driving(n2e[i], here, n2e[i + 2], slow, c[i + 2], th[i + 2], masks)
            fr = relaxing(here, slow, rc[i + 2])
            jump_e += (-7.0 / 24.0) * f0e[i + 2] + (1.0 / 3.0) * f1e[i + 1] - (1.0 / 24.0) * fe
            jump_r += (-7.0 / 24.0) * f0r[i + 2] + (1.0 / 3.0) * f1r[i + 1] - (1.0 / 24.0) * fr
            sum_e += (-1.0 / 24.0) * f0e[i + 2] + (1.0 / 3.0) * f1e[i + 1] + (5.0 / 24.0) * fe
            sum_r += (-1.0 / 24.0) * f0r[i + 2] + (1.0 / 3.0) * f1r[i + 1] + (5.0 / 24.0) * fr
        d1e[k] = pair_mean(jump_e, row)
        d1r[k] = pair_mean(jump_r, row)
        rse[k] = pair_mean(sum_e, row)
        rsr[k] = pair_mean(sum_r, row)

    loop(6, three)

    def four(k):
        i = 2 * k
        mean = lambda ref, at: pair_mean(ref[at + i] + ref[at + i + 1], row)
        gc, gt, gr = mean(c, 4), mean(th, 4), mean(rc, 4)
        be, br = mean(n1e, 4), mean(n1r, 4)
        de, dr = d1e[k + 1], d1r[k + 1]
        ce, cr = be + de, br + dr
        lap = coarse_laplace_inside(de, masks) + 0.25 * (d1e[k] + d1e[k + 2])
        ge = gc * lap + 2.0 * (ce * (1.0 - ce) * (ce - gt) - be * (1.0 - be) * (be - gt)) - dr
        g_r = gr * (de - 0.5 * dr)
        xe = ce + H * ge + rse[k + 1] - mean(n2e, 3)
        xr = cr + H * g_r + rsr[k + 1] - mean(n2r, 3)
        dle[k] = xe
        dlr[k] = xr
        for half in range(2):
            u2[0, i + half] = n2e[i + 3 + half] + xe
            u2[1, i + half] = n2r[i + 3 + half] + xr

    loop(4, four)

    def edges(right, pay, with_d):
        lo = 5 if right else 0
        if with_d:
            copy_planes(dpay, 0, u2.at[0], 5 if right else 0, 3)
            copy_planes(dpay, 3, u2.at[1], 6 if right else 0, 2)
        picks = (
            ((d1e, 3), (dle, 2), (dle, 3), (dlr, 3)) if right else ((d1e, 2), (dle, 0), (dle, 1), (dlr, 0))
        )
        for at, (ref, k) in enumerate(picks):
            pay[at] = ref[k, pl.ds(0, ROWS, stride=2), :]

    @pl.when(core == 0)
    def _():
        edges(True, apay, False)
        edges(False, bpay, True)

    @pl.when(core == 1)
    def _():
        edges(False, apay, False)
        edges(True, bpay, True)


def doubled(dst, k, src, at):
    v = src[at]
    dst[k, pl.ds(0, ROWS, stride=2), :] = v
    dst[k, pl.ds(1, ROWS, stride=2), :] = v


def middle_kernel(
    core_ref, ra, rb, c, th, rc, f0e, f0r, n1e, n1r, n2e, n2r, d1e, d1r, dle, dlr,
    k1e, k1r, k2e, k2r,
    u1e, u1r, u2e, u2r, xd1e, xdle, xdlr,
):
    core = core_ref[0]
    masks = grid_masks()
    copy_planes(xd1e, 1, d1e, 0, 6)
    copy_planes(xdle, 2, dle, 0, 4)
    copy_planes(xdlr, 1, dlr, 0, 4)

    def fill(left, right):
        doubled(xd1e, 0, left, 0)
        doubled(xdle, 0, left, 1)
        doubled(xdle, 1, left, 2)
        doubled(xdlr, 0, left, 3)
        doubled(xd1e, 7, right, 0)
        doubled(xdle, 6, right, 1)
        doubled(xdle, 7, right, 2)
        doubled(xdlr, 5, right, 3)

    sides(core, ra, rb, fill)

    def states_e(i):
        k = (i + 1) // 2
        u1e[i] = n1e[i + 1] + xd1e[k]
        u2e[i] = n2e[i] + xdle[k]

    loop(14, states_e)

    def states_r(i):
        k = i // 2
        u1r[i] = n1r[i + 2] + d1r[k]
        u2r[i] = n2r[i + 1] + xdlr[k]

    loop(12, states_r)

    def terms(i):
        fe = (
            driving(u1e[i], u1e[i + 1], u1e[i + 2], u1r[i], c[i + 2], th[i + 2], masks),
            driving(u2e[i], u2e[i + 1], u2e[i + 2], u2r[i], c[i + 2], th[i + 2], masks),
        )
        fr = (relaxing(u1e[i + 1], u1r[i], rc[i + 2]), relaxing(u2e[i + 1], u2r[i], rc[i + 2]))
        for f0, f, k1, k2 in ((f0e, fe, k1e, k2e), (f0r, fr, k1r, k2r)):
            base = f0[i + 2]
            k1[i] = (-7.0 / 24.0) * base + (1.0 / 3.0) * f[0] - (1.0 / 24.0) * f[1]
            k2[i] = (-1.0 / 24.0) * base - (1.0 / 6.0) * f[0] + (5.0 / 24.0) * f[1]

    loop(12, terms)


def edge_kernel(core_ref, q, pay):
    @pl.when(core_ref[0] == 0)
    def _():
        copy_planes(pay, 0, q.at[0], 5, 3)
        copy_planes(pay, 3, q.at[1], 6, 2)

    @pl.when(core_ref[0] == 1)
    def _():
        copy_planes(pay, 0, q.at[0], 0, 3)
        copy_planes(pay, 3, q.at[1], 0, 2)


def second_kernel(
    core_ref, head_ref, q, qa, qb, e, r, c, th, rc, k1e, k1r, k2e, k2r,
    apay, bpay, base, d1e, coef,
    qe, qr, fqe, fqr, n1e, n1r, f1e, f1r, n2e, n2r, d1r, rse, rsr,
):
    core = core_ref[0]
    masks = grid_masks()
    row = masks[0]

    @pl.when(head_ref[0] == 1)
    def _():
        copy_planes(qe, 0, e, 2, 14)
        copy_planes(qr, 0, r, 2, 12)

    @pl.when(head_ref[0] == 0)
    def _():
        copy_planes(qe, 3, q.at[0], 0, SLAB)
        copy_planes(qr, 2, q.at[1], 0, SLAB)

        def fill(left, right):
            copy_planes(qe, 0, left, 0, 3)
            copy_planes(qr, 0, left, 3, 2)
            copy_planes(qe, 11, right, 0, 3)
            copy_planes(qr, 10, right, 3, 2)

        sides(core, qa, qb, fill)

    def one(i):
        here, slow = qe[i + 1], qr[i]
        fe = driving(qe[i], here, qe[i + 2], slow, c[i + 2], th[i + 2], masks)
        fr = relaxing(here, slow, rc[i + 2])
        fqe[i] = fe
        fqr[i] = fr
        n1e[i] = here + H * fe + k1e[i]
        n1r[i] = slow + H * fr + k1r[i]

    loop(12, one)

    def two(i):
        here, slow = n1e[i + 1], n1r[i + 1]
        fe = driving(n1e[i], here, n1e[i + 2], slow, c[i + 3], th[i + 3], masks)
        fr = relaxing(here, slow, rc[i + 3])
        f1e[i] = fe
        f1r[i] = fr
        n2e[i] = here + H * fe + k2e[i + 1]
        n2r[i] = slow + H * fr + k2r[i + 1]

    loop(10, two)

    def three(k):
        jump_e = jump_r = sum_e = sum_r = 0.0
        for half in range(2):
            i = 2 * k + half
            here, slow = n2e[i + 1], n2r[i + 1]
            fe = driving(n2e[i], here, n2e[i + 2], slow, c[i + 4], th[i + 4], masks)
            fr = relaxing(here, slow, rc[i + 4])
            fq, f1 = fqe[i + 2], f1e[i + 1]
            jump_e += (qe[i + 3] - n1e[i + 2]) + (5.0 / 24.0) * fq + (1.0 / 3.0) * f1 - (1.0 / 24.0) * fe
            sum_e += (-1.0 / 24.0) * fq + (1.0 / 3.0) * f1 + (5.0 / 24.0) * fe
            fq, f1 = fqr[i + 2], f1r[i + 1]
            jump_r += (qr[i + 2] - n1r[i + 2]) + (5.0 / 24.0) * fq + (1.0 / 3.0) * f1 - (1.0 / 24.0) * fr
            sum_r += (-1.0 / 24.0) * fq + (1.0 / 3.0) * f1 + (5.0 / 24.0) * fr
        d1e[k + 1] = pair_mean(jump_e, row)
        d1r[k] = pair_mean(jump_r, row)
        rse[k] = pair_mean(sum_e, row)
        rsr[k] = pair_mean(sum_r, row)

    loop(4, three)
    d1e[0] = jnp.zeros(PLANE, F32)
    d1e[5] = jnp.zeros(PLANE, F32)

    @pl.when(core == 0)
    def _():
        apay[0] = d1e[4, pl.ds(0, ROWS, stride=2), :]
        bpay[0] = d1e[1, pl.ds(0, ROWS, stride=2), :]

    @pl.when(core == 1)
    def _():
        apay[0] = d1e[1, pl.ds(0, ROWS, stride=2), :]
        bpay[0] = d1e[4, pl.ds(0, ROWS, stride=2), :]

    def four(k):
        i = 2 * k
        mean = lambda ref, at: pair_mean(ref[at + i] + ref[at + i + 1], row)
        gc, gt, gr = mean(c, 4), mean(th, 4), mean(rc, 4)
        be, br = mean(n1e, 2), mean(n1r, 2)
        de, dr = d1e[k + 1], d1r[k]
        ce, cr = be + de, br + dr
        lap = coarse_laplace_inside(de, masks) + 0.25 * (d1e[k] + d1e[k + 2])
        ge = gc * lap + 2.0 * (ce * (1.0 - ce) * (ce - gt) - be * (1.0 - be) * (be - gt)) - dr
        g_r = gr * (de - 0.5 * dr)
        xe = ce + H * ge + rse[k] - mean(n2e, 1)
        xr = cr + H * g_r + rsr[k] - mean(n2r, 1)
        coef[k] = (0.25 * H) * gc
        for half in range(2):
            base[0, i + half] = n2e[i + 1 + half] + xe
            base[1, i + half] = n2r[i + 1 + half] + xr

    loop(4, four)


def last_kernel(core_ref, base, coef, ra, rb, out, wide):
    def fill(left, right):
        doubled(wide, 0, left, 0)
        doubled(wide, 1, right, 0)

    sides(core_ref[0], ra, rb, fill)
    out[0] = base[...]
    for side, k in ((0, 0), (1, 3)):
        add = coef[k] * wide[side]
        for half in range(2):
            out[0, 0, 2 * k + half] = base[0, 2 * k + half] + add


def call(kernel, out_shape, scratch=(), in_specs=None, out_specs=None, **kw):
    return pl.pallas_call(
        kernel,
        out_shape=out_shape,
        in_specs=in_specs,
        out_specs=out_specs,
        scratch_shapes=[pltpu.VMEM(s, F32) if isinstance(s, tuple) else s for s in scratch],
        compiler_params=pltpu.CompilerParams(vmem_limit_bytes=24 << 20),
        **kw,
    )


def per_device(start, conduct, threshold, recovery):
    steps = lax.axis_size("tm")
    space = lax.axis_size("space")
    place = lax.axis_index("space")
    core = (place % 2).reshape(1).astype(jnp.int32)
    head = (lax.axis_index("tm") == 0).reshape(1).astype(jnp.int32)

    chip_pairs = [(s, s ^ 1) for s in range(space)]
    link_pairs = [(s, s + 1) for s in range(1, space - 1, 2)] + [(s + 1, s) for s in range(1, space - 1, 2)]
    next_pairs = [(p, p + 1) for p in range(steps - 1)]
    slant_pairs = [(p * space + a, (p + 1) * space + b) for p in range(steps - 1) for a, b in link_pairs]
    on_chip = lambda v: lax.ppermute(v, "space", chip_pairs)
    on_link = lambda v: lax.ppermute(v, "space", link_pairs)

    to_a, to_b = call(
        pack_kernel,
        (planes(20), planes(20)),
        [pltpu.SemaphoreType.DMA((10,))],
        in_specs=[SM, ANY, ANY, ANY, ANY],
        out_specs=(VM, VM),
    )(core, start, conduct, threshold, recovery)
    got_b = on_link(to_b)
    got_a = on_chip(to_a)

    (u2, dpay, bpay, apay, e, r, c, th, rc, f0e, f0r, n1e, n1r, n2e, n2r, d1e, d1r, dle, dlr) = call(
        first_kernel,
        (jax.ShapeDtypeStruct((2, SLAB) + PLANE, F32), planes(5), planes(4, ROWS), planes(4, ROWS))
        + (planes(18), planes(16), planes(16), planes(16), planes(16))
        + (planes(16),) * 4
        + (planes(14),) * 2
        + (planes(6),) * 2
        + (planes(4),) * 2,
        [(14,) + PLANE] * 2 + [(6,) + PLANE] * 2 + [PLANE],
        in_specs=[SM] + [VM] * 6,
        out_specs=(VM,) * 19,
    )(core, start, conduct, threshold, recovery, got_a, got_b)

    q = lax.ppermute(u2, "tm", next_pairs)
    q_b = lax.ppermute(dpay, ("tm", "space"), slant_pairs)
    fix_b = on_link(bpay)
    fix_a = on_chip(apay)

    k_terms = call(
        middle_kernel,
        (planes(12),) * 4,
        [(14,) + PLANE, (12,) + PLANE] * 2 + [(8,) + PLANE] * 2 + [(6,) + PLANE],
        in_specs=[SM] + [VM] * 15,
        out_specs=(VM,) * 4,
    )(core, fix_a, fix_b, c, th, rc, f0e, f0r, n1e, n1r, n2e, n2r, d1e, d1r, dle, dlr)

    q_pay = call(edge_kernel, planes(5), in_specs=[SM, VM], out_specs=VM)(core, q)
    q_a = on_chip(q_pay)

    apay, bpay, base, d1, coef = call(
        second_kernel,
        (planes(1, ROWS), planes(1, ROWS), jax.ShapeDtypeStruct((2, SLAB) + PLANE, F32), planes(6), planes(4)),
        [(14,) + PLANE] + [(12,) + PLANE] * 5 + [(10,) + PLANE] * 4 + [(4,) + PLANE] * 3,
        in_specs=[SM, SM] + [VM] * 12,
        out_specs=(VM,) * 5,
    )(core, head, q, q_a, q_b, e, r, c, th, rc, *k_terms)

    jump_b = on_link(bpay)
    jump_a = on_chip(apay)
    return call(
        last_kernel,
        jax.ShapeDtypeStruct((1, 2, SLAB) + PLANE, F32),
        [(2,) + PLANE],
        in_specs=[SM] + [VM] * 4,
        out_specs=VM,
    )(core, base, coef, jump_a, jump_b)


def solution(mesh):
    placed = (
        P("tm", None, "space", None, None),
        P("space", None, None),
        P("space", None, None),
        P("space", None, None),
    )
    return jax.shard_map(
        per_device,
        mesh=mesh,
        in_specs=placed,
        out_specs=P("tm", None, "space", None, None),
        check_vma=False,
    )
```
